256 devices in a mesh: band: 16 (over z_lo, x), slab: 16 (over y, z_hi, core).
Axes of the slice: x: 4, y: 4, z: 8 (z_hi: 2, z_lo: 4; z = z_hi * 4 + z_lo), core: 2. Of those that a mesh axis runs over, the one named last changes fastest.
Arguments:
- orbitals: float32 [32, 128, 128, 128], P('band', 'slab'), may hold values from -6 to 6
- slot_ids: int32 [32], P('band'), may hold values from 0 to 31, each once
- occupations: float32 [32], replicated, may hold values from 0.25 to 2
- mode_lists: int32 [3, 48], replicated, may hold values from 0 to 127, as said below
Outputs:
- exchange_terms: float32 [32, 128, 128, 128], P('band', 'slab')
The draws below stay inside these ranges and needn't reach their ends.
Inputs may be any that keep to these rules, and one draw needn't show every extreme that they name: `slot_ids`: each number appears once. `mode_lists`: each row lists 48 different mode numbers, among them 0 and 127.
All inputs are finite; a program needn't handle non-finite values.
Results may differ from the reference program's by a relative error of at most 0.000059.
Values sent between devices are 32-bit elements; how exact they have to be, the bound alone decides.
No kernel may reach another device: no remote copies, remote signals or barrier semaphores. Data moves between devices by JAX's collectives and lax.ppermute only.
A program may use at most 64 MiB of HBM per device.

```python
import math
import jax
import jax.numpy as jnp
from jax import lax

NG = 128
KM = 48
ORBITALS = 32


def draw_mode_lists(key, part):
    listing = []
    for dimension in range(3):
        row_key = jax.random.fold_in(key, 17 + dimension)
        first_key, second_key = jax.random.split(row_key)
        inner = jax.random.permutation(first_key, NG - 2)[:KM - 2].astype(jnp.int32) + 1
        listed = jnp.concatenate([jnp.array([0, NG - 1], dtype=jnp.int32), inner])
        order = jax.random.permutation(second_key, KM)
        listing.append(listed[order])
    return jnp.stack(listing).astype(jnp.int32)


def block_levels(own_key, shape, cuts, least, largest):
    factor_of, own = 1.0, jax.random.fold_in(own_key, 6)
    for dim, parts in cuts:
        steps = jnp.exp(jax.random.uniform(jax.random.fold_in(own, dim), (parts,), jnp.float32, least / len(cuts), largest / len(cuts)))
        factor_of = factor_of * jnp.repeat(steps, shape[dim] // parts).reshape([-1 if axis == dim else 1 for axis in range(len(shape))])
    return factor_of


def centred(stream_key, dims, spread, bound, pieces=(), held_as=jnp.bfloat16):
    entries = spread * jax.random.normal(stream_key, dims, jnp.float32)
    if pieces:
        entries = entries * block_levels(stream_key, dims, pieces, -0.22, 0.18)
    return jnp.clip(entries, -bound, bound).astype(held_as)


def setup_inputs(seed: int = 0) -> dict:
    arg_keys = jax.random.split(jax.random.key(seed), 5)
    return {
        "orbitals": centred(arg_keys[0], (ORBITALS, NG, NG, NG), 1.0, 6.0, ((0, 16), (1, 16)), jnp.float32),
        "slot_ids": jax.random.permutation(arg_keys[1], ORBITALS).astype(jnp.int32),
        "occupations": jnp.clip(jnp.exp(jax.random.uniform(arg_keys[2], (ORBITALS,), jnp.float32, math.log(0.25), math.log(2.0))), 0.25, 2.0),
        "mode_lists": draw_mode_lists(jax.random.fold_in(arg_keys[4], 71), 0),
    }


def sine_table(mode_row, points):
    grid = jnp.arange(points, dtype=jnp.int32) + 1
    phase = grid[:, None] * (mode_row[None, :].astype(jnp.int32) + 1) % (2 * points + 2)
    angle = jnp.pi * phase.astype(jnp.float32) / (points + 1.0)
    return jnp.sqrt(jnp.float32(2.0) / (points + 1.0)) * jnp.sin(angle)

def screen_table(first, second, third, points):
    squares = ((first + 1) ** 2)[:, None, None] + ((second + 1) ** 2)[None, :, None] + ((third + 1) ** 2)[None, None, :]
    return 1.0 / (1.0 + squares.astype(jnp.float32) / jnp.float32(points * points))

def reference(orbitals, slot_ids, occupations, mode_lists):
    highest = lax.Precision.HIGHEST
    slot_weight = occupations[slot_ids]
    sine_first = sine_table(mode_lists[0], NG)
    sine_second = sine_table(mode_lists[1], NG)
    sine_third = sine_table(mode_lists[2], NG)
    screen = screen_table(mode_lists[0], mode_lists[1], mode_lists[2], NG)

    def one_slot(index):
        density = orbitals[index][None] * orbitals
        coeff = jnp.einsum('jxyz,zc->jxyc', density, sine_third, precision=highest)
        coeff = jnp.einsum('jxyc,yb->jxbc', coeff, sine_second, precision=highest)
        coeff = jnp.einsum('jxbc,xa->jabc', coeff, sine_first, precision=highest)
        coeff = coeff * screen[None]
        field = jnp.einsum('jabc,xa->jxbc', coeff, sine_first, precision=highest)
        field = jnp.einsum('jxbc,yb->jxyc', field, sine_second, precision=highest)
        field = jnp.einsum('jxyc,zc->jxyz', field, sine_third, precision=highest)
        return lax.optimization_barrier(jnp.sum(slot_weight[:, None, None, None] * orbitals * field, axis=0))
    return lax.map(one_slot, jnp.arange(orbitals.shape[0], dtype=jnp.int32))
```

```python
import functools

import jax
import jax.numpy as jnp
from jax import lax
from jax.experimental import pallas as pl
from jax.experimental.pallas import tpu as pltpu
from jax.sharding import Mesh
from jax.sharding import PartitionSpec as P


MODES = ("y", "core")
BLOCK = 2


def sine_table(left, right, points):
    phase = (left[:, None] + 1) * (right[None, :] + 1) % (2 * points + 2)
    angle = jnp.pi * phase.astype(jnp.float32) / (points + 1.0)
    return jnp.sqrt(jnp.float32(2.0) / (points + 1.0)) * jnp.sin(angle)


def screen_table(first, second, third, points):
    squares = (
        ((first + 1) ** 2)[:, None, None]
        + ((second + 1) ** 2)[None, :, None]
        + ((third + 1) ** 2)[None, None, :]
    )
    return 1.0 / (1.0 + squares.astype(jnp.float32) / jnp.float32(points * points))


def halves(value):
    high = value.astype(jnp.bfloat16)
    low = (value - high.astype(jnp.float32)).astype(jnp.bfloat16)
    return high, low


def table_halves(value):
    high = lax.reduce_precision(value, exponent_bits=8, mantissa_bits=7)
    return high.astype(jnp.bfloat16), (value - high).astype(jnp.bfloat16)


def dot3(left, right):
    mul = functools.partial(jnp.dot, preferred_element_type=jnp.float32)
    return mul(left[0], right[0]) + (mul(left[1], right[0]) + mul(left[0], right[1]))


def window(step, count, pairs=2):
    first = 2 * step * count // 128 * 128
    last = (2 * step + pairs) * count
    return first, -(-(last - first) // 128) * 128


def lanes_of(pairs, count):
    return -(-len(pairs) * count // 128) * 128


def loaded(refs, flags, spot):
    if len(spot) == 2:
        return refs[spot[0]][spot[1]]
    flag, (a, i), (b, j) = spot
    return jnp.where(flags[flag] != 0, refs[a][i], refs[b][j])


def added(refs, flags, spot, term):
    if len(spot) == 2:
        refs[spot[0]][spot[1]] += term
    else:
        flag, (a, i), (b, j) = spot
        chosen = flags[flag] != 0
        refs[a][i] += jnp.where(chosen, term, 0.0)
        refs[b][j] += jnp.where(chosen, 0.0, term)


def forward_kernel(pairs, count, n_arrays, flags, *refs):
    arrays = refs[:n_arrays]
    wide_hi, wide_lo, flip_hi, flip_lo, out = refs[n_arrays:]
    points = wide_hi.shape[1] // 2
    tall = out.shape[0] // count
    tiles = [None] * (tall // 8)
    for step in range(-(-len(pairs) // 2)):
        couple = pairs[2 * step : 2 * step + 2]
        parts = [
            (loaded(arrays, flags, f) * loaded(arrays, flags, s)).reshape(-1, points)
            for f, s in couple
        ]
        density = parts[0] if len(parts) == 1 else jnp.concatenate(parts, axis=1)
        deep = density.shape[1]
        first, width = window(step, count, len(parts))
        made = dot3(
            halves(density), (wide_hi[step % 4, :deep, :width], wide_lo[step % 4, :deep, :width])
        )
        for part in range(width // 128):
            tile = first // 128 + part
            piece = made[:, part * 128 : part * 128 + 128]
            tiles[tile] = piece if tiles[tile] is None else tiles[tile] + piece
    whole = jnp.concatenate(tiles, axis=1)
    flip = (flip_hi[...], flip_lo[...])
    for plane in range(BLOCK):
        made = dot3(flip, halves(whole[plane * points : (plane + 1) * points]))
        for tile in range(len(tiles)):
            start = tile * 8 + pl.program_id(0) * BLOCK + plane
            out[pl.ds(start, count, stride=tall), :] = made[:, tile * 128 : tile * 128 + 128]


def inverse_kernel(pairs, count, n_arrays, had, flags, *refs):
    arrays = refs[:n_arrays]
    before = refs[n_arrays : n_arrays + sum(had)]
    given, tall_hi, tall_lo, back_hi, back_lo = refs[n_arrays + sum(had) :][:5]
    outs = refs[n_arrays + sum(had) + 5 :]
    points = back_hi.shape[0]
    tall = given.shape[0] // count
    taken = iter(before)
    for out, old in zip(outs, had):
        out[...] = next(taken)[...] if old else jnp.zeros_like(out)
    back = (back_hi[...], back_lo[...])
    planes = []
    for plane in range(BLOCK):
        start = pl.program_id(0) * BLOCK + plane
        got = [given[pl.ds(tile + start, count, stride=tall), :] for tile in range(0, tall, 8)]
        planes.append(dot3(back, halves(jnp.concatenate(got, axis=1))))
    high, low = halves(jnp.concatenate(planes, axis=0))
    for step in range(-(-len(pairs) // 2)):
        couple = pairs[2 * step : 2 * step + 2]
        first, width = window(step, count, len(couple))
        wide = 128 * len(couple)
        field = dot3(
            (high[:, first : first + width], low[:, first : first + width]),
            (tall_hi[step % 4, :width, :wide], tall_lo[step % 4, :width, :wide]),
        )
        for place, (f, s) in enumerate(couple):
            piece = field[:, place * 128 : place * 128 + 128].reshape(BLOCK, points, points)
            added(outs, flags, f, loaded(arrays, flags, s) * piece)
            if f != s:
                added(outs, flags, s, loaded(arrays, flags, f) * piece)


def slab_spec(array):
    return pl.BlockSpec((array.shape[0], BLOCK) + array.shape[2:], lambda x: (0, x, 0, 0))


def whole_spec(array):
    return pl.BlockSpec(array.shape, lambda x: (0,) * array.ndim)


SCALARS = pl.BlockSpec(memory_space=pltpu.SMEM)


def forward(arrays, pairs, tables):
    count = tables["flip"][0].shape[0]
    planes, points = arrays[0].shape[1:3]
    lanes = lanes_of(pairs, count)
    fixed = [*tables["wide"], *tables["flip"]]
    flops = len(pairs) * planes * points * (points + count) * count * 6
    return pl.pallas_call(
        functools.partial(forward_kernel, pairs, count, len(arrays)),
        grid=(planes // BLOCK,),
        in_specs=[SCALARS] + [slab_spec(a) for a in arrays] + [whole_spec(a) for a in fixed],
        out_specs=pl.BlockSpec((count * planes * lanes // 128, 128), lambda x: (0, 0)),
        out_shape=jax.ShapeDtypeStruct((count * planes * lanes // 128, 128), jnp.float32),
        cost_estimate=pl.CostEstimate(flops=8 * flops, transcendentals=0, bytes_accessed=8 << 20),
        name="pairs_forward",
    )(tables["flags"], *arrays, *fixed)


def inverse(given, arrays, pairs, before, tables):
    count = tables["flip"][0].shape[0]
    planes, points = arrays[0].shape[1:3]
    fixed = [given, *tables["tall"], *tables["back"]]
    had = tuple(b is not None for b in before)
    olds = [b for b in before if b is not None]
    flops = len(pairs) * planes * points * (points + count) * count * 6
    return pl.pallas_call(
        functools.partial(inverse_kernel, pairs, count, len(arrays), had),
        grid=(planes // BLOCK,),
        in_specs=[SCALARS]
        + [slab_spec(a) for a in [*arrays, *olds]]
        + [whole_spec(a) for a in fixed],
        out_specs=[slab_spec(a) for a in arrays],
        out_shape=[jax.ShapeDtypeStruct(a.shape, jnp.float32) for a in arrays],
        cost_estimate=pl.CostEstimate(flops=8 * flops, transcendentals=0, bytes_accessed=12 << 20),
        name="pairs_inverse",
    )(tables["flags"], *arrays, *olds, *fixed)


def spectral_kernel(given, turned_hi, turned_lo, out):
    groups, share, tiles, planes, wide = given.shape
    turned = (turned_hi[...], turned_lo[...])
    for mode in range(share):
        blocks = [given[:, mode, t].reshape(groups * planes, wide) for t in range(tiles)]
        made = dot3(turned, halves(jnp.concatenate(blocks, axis=1)))
        for t in range(tiles):
            out[mode, t] = made[:, t * wide : (t + 1) * wide]


def spatial_kernel(here, other, screen, first_hi, first_lo, out):
    groups, share, tiles, planes, wide = out.shape
    first = (first_hi[...], first_lo[...])
    for mode in range(share):
        parts = [(here[mode, t] + other[mode, t]) * screen[mode, t] for t in range(tiles)]
        made = dot3(first, halves(jnp.concatenate(parts, axis=1)))
        for t in range(tiles):
            out[:, mode, t] = made[:, t * wide : (t + 1) * wide].reshape(groups, planes, wide)


def to_spectral(given, tables):
    share, tiles = given.shape[1:3]
    count, rows = tables["turned"][0].shape
    return pl.pallas_call(
        spectral_kernel,
        out_shape=jax.ShapeDtypeStruct((share, tiles, count, 128), jnp.float32),
        cost_estimate=pl.CostEstimate(
            flops=40 * rows * count * share * tiles * 128,
            transcendentals=0,
            bytes_accessed=8 * given.size,
        ),
        name="to_spectral",
    )(given, *tables["turned"])


def to_spatial(here, other, shape, tables):
    share, tiles, count, _ = here.shape
    rows = tables["first"][0].shape[0]
    return pl.pallas_call(
        spatial_kernel,
        out_shape=jax.ShapeDtypeStruct(shape, jnp.float32),
        cost_estimate=pl.CostEstimate(
            flops=40 * rows * count * share * tiles * 128,
            transcendentals=0,
            bytes_accessed=12 * here.size,
        ),
        name="to_spatial",
    )(here, other, tables["screen"], *tables["first"])


def make_tables(mode_lists, points):
    count = mode_lists.shape[1]
    share = count // lax.axis_size(MODES)
    grid = jnp.arange(points, dtype=jnp.int32)
    third = sine_table(grid, mode_lists[2], points)
    third_turned = sine_table(mode_lists[2], grid, points)
    here = grid.reshape(lax.axis_size("y"), lax.axis_size("z_hi"), -1)
    here = lax.dynamic_index_in_dim(here, lax.axis_index("z_hi"), 1, keepdims=False).reshape(-1)
    local = lax.dynamic_slice_in_dim(mode_lists[1], lax.axis_index(MODES) * share, share)
    screen = screen_table(local, mode_lists[0], mode_lists[2], points)
    screen = jnp.tile(screen, (1, 1, 16)).reshape(share, count, -1, 128).transpose(0, 2, 1, 3)
    wide = []
    tall = []
    for step in range(4):
        offset = 2 * step * count - window(step, count)[0]
        rest = 256 - offset - count
        wide.append(
            jnp.pad(third, ((0, points), (offset, rest)))
            + jnp.pad(third, ((points, 0), (offset + count, rest - count)))
        )
        tall.append(
            jnp.pad(third_turned, ((offset, rest), (0, points)))
            + jnp.pad(third_turned, ((offset + count, rest - count), (points, 0)))
        )
    return {
        "wide": table_halves(jnp.stack(wide)),
        "tall": table_halves(jnp.stack(tall)),
        "flip": table_halves(sine_table(mode_lists[1], grid, points)),
        "back": table_halves(sine_table(grid, mode_lists[1], points)),
        "first": table_halves(sine_table(here, mode_lists[0], points)),
        "turned": table_halves(sine_table(mode_lists[0], here, points)),
        "screen": screen,
    }


def moved(value, axis, steps):
    size = lax.axis_size(axis)
    pairs = [((place + steps) % size, place) for place in range(size)]
    return lax.ppermute(value, axis, pairs)


def on_device(orbitals, slot_ids, occupations, mode_lists):
    planes, points = orbitals.shape[1:3]
    groups = lax.axis_size(MODES)
    count = mode_lists.shape[1]
    share = count // groups
    catalog = jnp.arange(occupations.shape[0], dtype=jnp.int32)
    weight = jnp.sum(
        jnp.where(slot_ids[:, None] == catalog[None, :], occupations[None, :], 0.0), axis=1
    )
    root = jnp.sqrt(weight)[:, None, None, None]
    o = orbitals * root
    v = moved(o, "z_lo", 1)
    a = moved(o, "x", 1)
    c = moved(o, "x", -1)
    w = moved(v, "z_lo", 1)
    tables = make_tables(mode_lists, points)
    sides = [lax.axis_index(n) < lax.axis_size(n) // 2 for n in ("x", "z_lo")]
    tables["flags"] = jnp.stack(sides).astype(jnp.int32)
    tables, a = lax.optimization_barrier((tables, a))
    b = moved(a, "x", 1)
    arrays = {"o": o, "a": a, "b": b, "c": c, "v": v, "w": w}
    chosen = {
        "p0": (0, "o0", "b1"),
        "p1": (0, "b0", "o0"),
        "p2": (0, "b1", "o1"),
        "d0": (1, "o0", "b0"),
        "d1": (1, "o1", "b1"),
    }

    def product(first, second):
        return [(first + i, second + j) for i in "01" for j in "01"]

    chunks = [
        product("v", "a") + product("v", "c") + product("o", "a") + [("o0", "o1")],
        product("w", "a") + product("w", "d") + [("o0", "o0"), ("o1", "o1")],
        product("v", "o") + product("v", "b") + [("p0", "p1"), ("p0", "p2")],
    ]

    def parts(name):
        return chosen[name][1:] if name in chosen else (name,)

    names = [
        sorted({part[0] for pair in chunk for name in pair for part in parts(name)})
        for chunk in chunks
    ]

    def spot(k, name):
        if name in chosen:
            flag, first, second = chosen[name]
            return (flag, spot(k, first), spot(k, second))
        return (names[k].index(name[0]), int(name[1]))

    indexed = [[tuple(spot(k, n) for n in pair) for pair in chunk] for k, chunk in enumerate(chunks)]

    def exchange(value):
        return lax.all_to_all(value, MODES, split_axis=0, concat_axis=0, tiled=True)

    def pairs_there(k):
        made = forward([arrays[n] for n in names[k]], indexed[k], tables)
        return exchange(made.reshape(groups, share, -1, planes, 128))

    def swapped(got):
        here = to_spectral(got, tables)
        return here, moved(here, "z_hi", 1)

    sums = {}

    def collect(k, here, other, shape):
        field = to_spatial(here, other, shape, tables)
        field = exchange(field).reshape(-1, 128)
        before = [sums.get(n) for n in names[k]]
        taken = [arrays[n] for n in names[k]]
        made = inverse(field, taken, indexed[k], before, tables)
        sums.update(zip(names[k], made))

    got = [pairs_there(k) for k in range(3)]
    here0, other0 = swapped(got[0])
    here1, other1 = swapped(got[1])
    here2 = to_spectral(got[2], tables)
    here2, other1 = lax.optimization_barrier((here2, other1))
    other2 = moved(here2, "z_hi", 1)
    collect(0, here0, other0, got[0].shape)
    collect(1, here1, other1, got[1].shape)
    sums["w"], other2 = lax.optimization_barrier((sums["w"], other2))
    home = [moved(sums["a"], "x", -1), moved(sums["c"], "x", 1)]
    to_v = moved(sums["w"], "z_lo", -1)
    collect(2, here2, other2, got[2].shape)
    home += [moved(sums["b"], "x", -2), moved(sums["v"] + to_v, "z_lo", -1)]
    total = sums["o"]
    for part in home:
        total = total + part
    return total / root


def solution(mesh):
    names = ("z_lo", "x", "y", "z_hi", "core")
    fine = Mesh(mesh.devices.reshape(4, 4, 4, 2, 2), names)
    placed = P(names[:2], names[2:], None, None)
    in_specs = (placed, P(names[:2]), P(), P())

    return jax.shard_map(on_device, mesh=fine, in_specs=in_specs, out_specs=placed, check_vma=False)
```

```python
import functools

import jax
import jax.numpy as jnp
from jax import lax
from jax.experimental import pallas as pl
from jax.experimental.pallas import tpu as pltpu
from jax.sharding import Mesh
from jax.sharding import PartitionSpec as P


MODES = ("y", "core")
BLOCK = 4


def sine_table(left, right, points):
    phase = (left[:, None] + 1) * (right[None, :] + 1) % (2 * points + 2)
    angle = jnp.pi * phase.astype(jnp.float32) / (points + 1.0)
    return jnp.sqrt(jnp.float32(2.0) / (points + 1.0)) * jnp.sin(angle)


def screen_table(first, second, third, points):
    squares = (
        ((first + 1) ** 2)[:, None, None]
        + ((second + 1) ** 2)[None, :, None]
        + ((third + 1) ** 2)[None, None, :]
    )
    return 1.0 / (1.0 + squares.astype(jnp.float32) / jnp.float32(points * points))


def halves(value):
    high = value.astype(jnp.bfloat16)
    low = (value - high.astype(jnp.float32)).astype(jnp.bfloat16)
    return high, low


def table_halves(value):
    high = lax.reduce_precision(value, exponent_bits=8, mantissa_bits=7)
    return high.astype(jnp.bfloat16), (value - high).astype(jnp.bfloat16)


def stacked_halves(value):
    return jnp.concatenate(table_halves(value), axis=0)


def table_dot(stacked, value):
    high, low = halves(value)
    rows = stacked.shape[0] // 2
    both = jnp.dot(stacked[...], high, preferred_element_type=jnp.float32)
    rest = jnp.dot(stacked[:rows], low, preferred_element_type=jnp.float32)
    return both[:rows] + (both[rows:] + rest)


def wide_dot(left, right):
    width = right[0].shape[1]
    if width > 128:
        return dot3(left, right)
    mul = functools.partial(jnp.dot, preferred_element_type=jnp.float32)
    both = mul(left[0], jnp.concatenate(right, axis=1))
    return both[:, :width] + (both[:, width:] + mul(left[1], right[0]))


def deep_dot(left, right):
    if left[0].shape[1] > 128:
        return dot3(left, right)
    mul = functools.partial(jnp.dot, preferred_element_type=jnp.float32)
    both = mul(jnp.concatenate(left, axis=1), jnp.concatenate([right[0]] * 2, axis=0))
    return both + mul(left[0], right[1])


def triple_halves(value):
    high, low = table_halves(value)
    return jnp.concatenate([high, high, low], axis=1)


def triple_dot(tripled, value):
    high, low = halves(value)
    stacked = jnp.concatenate([high, low, high], axis=0)
    return jnp.dot(tripled[...], stacked, preferred_element_type=jnp.float32)


def dot3(left, right):
    mul = functools.partial(jnp.dot, preferred_element_type=jnp.float32)
    return mul(left[0], right[0]) + (mul(left[1], right[0]) + mul(left[0], right[1]))


def window(step, count, pairs=2):
    first = 2 * step * count // 128 * 128
    last = (2 * step + pairs) * count
    return first, -(-(last - first) // 128) * 128


def lanes_of(pairs, count):
    return -(-len(pairs) * count // 128) * 128


def loaded(refs, flags, spot):
    if len(spot) == 2:
        return refs[spot[0]][spot[1]]
    flag, (a, i), (b, j) = spot
    return jnp.where(flags[flag] != 0, refs[a][i], refs[b][j])


def added(refs, flags, spot, term):
    if len(spot) == 2:
        refs[spot[0]][spot[1]] += term
    else:
        flag, (a, i), (b, j) = spot
        chosen = flags[flag] != 0
        refs[a][i] += jnp.where(chosen, term, 0.0)
        refs[b][j] += jnp.where(chosen, 0.0, term)


def forward_kernel(pairs, count, n_arrays, flags, *refs):
    arrays = refs[:n_arrays]
    wide_hi, wide_lo, flip, out = refs[n_arrays:]
    points = wide_hi.shape[1] // 2
    tall = out.shape[0] // count
    tiles = [None] * (tall // 8)
    for step in range(-(-len(pairs) // 2)):
        couple = pairs[2 * step : 2 * step + 2]
        parts = [
            (loaded(arrays, flags, f) * loaded(arrays, flags, s)).reshape(-1, points)
            for f, s in couple
        ]
        density = parts[0] if len(parts) == 1 else jnp.concatenate(parts, axis=1)
        deep = density.shape[1]
        first, width = window(step, count, len(parts))
        made = wide_dot(
            halves(density), (wide_hi[step % 4, :deep, :width], wide_lo[step % 4, :deep, :width])
        )
        for part in range(width // 128):
            tile = first // 128 + part
            piece = made[:, part * 128 : part * 128 + 128]
            tiles[tile] = piece if tiles[tile] is None else tiles[tile] + piece
    whole = jnp.concatenate(tiles, axis=1)
    for plane in range(BLOCK):
        made = table_dot(flip, whole[plane * points : (plane + 1) * points])
        for tile in range(len(tiles)):
            start = tile * 8 + pl.program_id(0) * BLOCK + plane
            out[pl.ds(start, count, stride=tall), :] = made[:, tile * 128 : tile * 128 + 128]


def inverse_kernel(pairs, count, n_arrays, had, flags, *refs):
    arrays = refs[:n_arrays]
    before = refs[n_arrays : n_arrays + sum(had)]
    given, tall_hi, tall_lo, back = refs[n_arrays + sum(had) :][:4]
    outs = refs[n_arrays + sum(had) + 4 :]
    points = back.shape[0]
    tall = given.shape[0] // count
    taken = iter(before)
    for out, old in zip(outs, had):
        out[...] = next(taken)[...] if old else jnp.zeros_like(out)
    planes = []
    for plane in range(BLOCK):
        start = pl.program_id(0) * BLOCK + plane
        got = [given[pl.ds(tile + start, count, stride=tall), :] for tile in range(0, tall, 8)]
        planes.append(triple_dot(back, jnp.concatenate(got, axis=1)))
    high, low = halves(jnp.concatenate(planes, axis=0))
    for step in range(-(-len(pairs) // 2)):
        couple = pairs[2 * step : 2 * step + 2]
        first, width = window(step, count, len(couple))
        wide = 128 * len(couple)
        field = deep_dot(
            (high[:, first : first + width], low[:, first : first + width]),
            (tall_hi[step % 4, :width, :wide], tall_lo[step % 4, :width, :wide]),
        )
        for place, (f, s) in enumerate(couple):
            piece = field[:, place * 128 : place * 128 + 128].reshape(BLOCK, points, points)
            added(outs, flags, f, loaded(arrays, flags, s) * piece)
            if f != s:
                added(outs, flags, s, loaded(arrays, flags, f) * piece)


def slab_spec(array):
    return pl.BlockSpec((array.shape[0], BLOCK) + array.shape[2:], lambda x: (0, x, 0, 0))


def whole_spec(array):
    return pl.BlockSpec(array.shape, lambda x: (0,) * array.ndim)


SCALARS = pl.BlockSpec(memory_space=pltpu.SMEM)


def forward(arrays, pairs, tables):
    count = tables["flip"].shape[0] // 2
    planes, points = arrays[0].shape[1:3]
    lanes = lanes_of(pairs, count)
    fixed = [*tables["wide"], tables["flip"]]
    flops = len(pairs) * planes * points * (points + count) * count * 6
    return pl.pallas_call(
        functools.partial(forward_kernel, pairs, count, len(arrays)),
        grid=(planes // BLOCK,),
        in_specs=[SCALARS] + [slab_spec(a) for a in arrays] + [whole_spec(a) for a in fixed],
        out_specs=pl.BlockSpec((count * planes * lanes // 128, 128), lambda x: (0, 0)),
        out_shape=jax.ShapeDtypeStruct((count * planes * lanes // 128, 128), jnp.float32),
        cost_estimate=pl.CostEstimate(flops=8 * flops, transcendentals=0, bytes_accessed=8 << 20),
        name="pairs_forward",
    )(tables["flags"], *arrays, *fixed)


def inverse(given, arrays, pairs, before, tables):
    count = tables["flip"].shape[0] // 2
    planes, points = arrays[0].shape[1:3]
    fixed = [given, *tables["tall"], tables["back"]]
    had = tuple(b is not None for b in before)
    olds = [b for b in before if b is not None]
    flops = len(pairs) * planes * points * (points + count) * count * 6
    return pl.pallas_call(
        functools.partial(inverse_kernel, pairs, count, len(arrays), had),
        grid=(planes // BLOCK,),
        in_specs=[SCALARS]
        + [slab_spec(a) for a in [*arrays, *olds]]
        + [whole_spec(a) for a in fixed],
        out_specs=[slab_spec(a) for a in arrays],
        out_shape=[jax.ShapeDtypeStruct(a.shape, jnp.float32) for a in arrays],
        cost_estimate=pl.CostEstimate(flops=8 * flops, transcendentals=0, bytes_accessed=12 << 20),
        name="pairs_inverse",
    )(tables["flags"], *arrays, *olds, *fixed)


def spectral_kernel(given, turned, out):
    groups, share, tiles, planes, wide = given.shape
    for mode in range(share):
        blocks = [given[:, mode, t].reshape(groups * planes, wide) for t in range(tiles)]
        made = table_dot(turned, jnp.concatenate(blocks, axis=1))
        for t in range(tiles):
            out[mode, t] = made[:, t * wide : (t + 1) * wide]


def spatial_kernel(here, other, screen, first, out):
    groups, share, tiles, planes, wide = out.shape
    for mode in range(share):
        parts = [(here[mode, t] + other[mode, t]) * screen[mode, t] for t in range(tiles)]
        made = triple_dot(first, jnp.concatenate(parts, axis=1))
        for t in range(tiles):
            out[:, mode, t] = made[:, t * wide : (t + 1) * wide].reshape(groups, planes, wide)


def to_spectral(given, tables):
    share, tiles = given.shape[1:3]
    count, rows = given.shape[0] * share, given.shape[0] * given.shape[3]
    return pl.pallas_call(
        spectral_kernel,
        out_shape=jax.ShapeDtypeStruct((share, tiles, count, 128), jnp.float32),
        cost_estimate=pl.CostEstimate(
            flops=40 * rows * count * share * tiles * 128,
            transcendentals=0,
            bytes_accessed=8 * given.size,
        ),
        name="to_spectral",
    )(given, tables["turned"])


def to_spatial(here, other, shape, tables):
    share, tiles, count, _ = here.shape
    rows = shape[0] * shape[3]
    return pl.pallas_call(
        spatial_kernel,
        out_shape=jax.ShapeDtypeStruct(shape, jnp.float32),
        cost_estimate=pl.CostEstimate(
            flops=40 * rows * count * share * tiles * 128,
            transcendentals=0,
            bytes_accessed=12 * here.size,
        ),
        name="to_spatial",
    )(here, other, tables["screen"], tables["first"])


def make_tables(mode_lists, points):
    count = mode_lists.shape[1]
    share = count // lax.axis_size(MODES)
    grid = jnp.arange(points, dtype=jnp.int32)
    third = sine_table(grid, mode_lists[2], points)
    third_turned = sine_table(mode_lists[2], grid, points)
    here = grid.reshape(lax.axis_size("y"), lax.axis_size("z_hi"), -1)
    here = lax.dynamic_index_in_dim(here, lax.axis_index("z_hi"), 1, keepdims=False).reshape(-1)
    local = lax.dynamic_slice_in_dim(mode_lists[1], lax.axis_index(MODES) * share, share)
    screen = screen_table(local, mode_lists[0], mode_lists[2], points)
    screen = jnp.tile(screen, (1, 1, 16)).reshape(share, count, -1, 128).transpose(0, 2, 1, 3)
    wide = []
    tall = []
    for step in range(4):
        offset = 2 * step * count - window(step, count)[0]
        rest = 256 - offset - count
        wide.append(
            jnp.pad(third, ((0, points), (offset, rest)))
            + jnp.pad(third, ((points, 0), (offset + count, rest - count)))
        )
        tall.append(
            jnp.pad(third_turned, ((offset, rest), (0, points)))
            + jnp.pad(third_turned, ((offset + count, rest - count), (points, 0)))
        )
    return {
        "wide": table_halves(jnp.stack(wide)),
        "tall": table_halves(jnp.stack(tall)),
        "flip": stacked_halves(sine_table(mode_lists[1], grid, points)),
        "back": triple_halves(sine_table(grid, mode_lists[1], points)),
        "first": triple_halves(sine_table(here, mode_lists[0], points)),
        "turned": stacked_halves(sine_table(mode_lists[0], here, points)),
        "screen": screen,
    }


def moved(value, axis, steps):
    size = lax.axis_size(axis)
    pairs = [((place + steps) % size, place) for place in range(size)]
    return lax.ppermute(value, axis, pairs)


def on_device(orbitals, slot_ids, occupations, mode_lists):
    planes, points = orbitals.shape[1:3]
    groups = lax.axis_size(MODES)
    count = mode_lists.shape[1]
    share = count // groups
    catalog = jnp.arange(occupations.shape[0], dtype=jnp.int32)
    weight = jnp.sum(
        jnp.where(slot_ids[:, None] == catalog[None, :], occupations[None, :], 0.0), axis=1
    )
    root = jnp.sqrt(weight)[:, None, None, None]
    o = orbitals * root
    v = moved(o, "z_lo", 1)
    a = moved(o, "x", 1)
    c = moved(o, "x", -1)
    w = moved(v, "z_lo", 1)
    tables = make_tables(mode_lists, points)
    sides = [lax.axis_index(n) < lax.axis_size(n) // 2 for n in ("x", "z_lo")]
    tables["flags"] = jnp.stack(sides).astype(jnp.int32)
    tables, a = lax.optimization_barrier((tables, a))
    b = moved(a, "x", 1)
    arrays = {"o": o, "a": a, "b": b, "c": c, "v": v, "w": w}
    chosen = {
        "p0": (0, "o0", "b1"),
        "p1": (0, "b0", "o0"),
        "p2": (0, "b1", "o1"),
        "d0": (1, "o0", "b0"),
        "d1": (1, "o1", "b1"),
    }

    def product(first, second):
        return [(first + i, second + j) for i in "01" for j in "01"]

    chunks = [
        product("v", "a") + product("v", "c") + product("o", "a") + [("o0", "o1")],
        product("w", "a") + product("w", "d") + [("o0", "o0"), ("o1", "o1")],
        product("v", "o") + product("v", "b") + [("p0", "p1"), ("p0", "p2")],
    ]

    def parts(name):
        return chosen[name][1:] if name in chosen else (name,)

    names = [
        sorted({part[0] for pair in chunk for name in pair for part in parts(name)})
        for chunk in chunks
    ]

    def spot(k, name):
        if name in chosen:
            flag, first, second = chosen[name]
            return (flag, spot(k, first), spot(k, second))
        return (names[k].index(name[0]), int(name[1]))

    indexed = [[tuple(spot(k, n) for n in pair) for pair in chunk] for k, chunk in enumerate(chunks)]

    def exchange(value):
        return lax.all_to_all(value, MODES, split_axis=0, concat_axis=0, tiled=True)

    def pairs_there(k):
        made = forward([arrays[n] for n in names[k]], indexed[k], tables)
        return exchange(made.reshape(groups, share, -1, planes, 128))

    def swapped(got):
        here = to_spectral(got, tables)
        return here, moved(here, "z_hi", 1)

    sums = {}

    def collect(k, here, other, shape):
        field = to_spatial(here, other, shape, tables)
        field = exchange(field).reshape(-1, 128)
        before = [sums.get(n) for n in names[k]]
        taken = [arrays[n] for n in names[k]]
        made = inverse(field, taken, indexed[k], before, tables)
        sums.update(zip(names[k], made))

    got = [pairs_there(k) for k in range(3)]
    here0, other0 = swapped(got[0])
    here1, other1 = swapped(got[1])
    here2 = to_spectral(got[2], tables)
    here2, other1 = lax.optimization_barrier((here2, other1))
    other2 = moved(here2, "z_hi", 1)
    collect(0, here0, other0, got[0].shape)
    collect(1, here1, other1, got[1].shape)
    sums["w"], other2 = lax.optimization_barrier((sums["w"], other2))
    home = [moved(sums["a"], "x", -1), moved(sums["c"], "x", 1)]
    to_v = moved(sums["w"], "z_lo", -1)
    collect(2, here2, other2, got[2].shape)
    home += [moved(sums["b"], "x", -2), moved(sums["v"] + to_v, "z_lo", -1)]
    total = sums["o"]
    for part in home:
        total = total + part
    return total / root


def solution(mesh):
    names = ("z_lo", "x", "y", "z_hi", "core")
    fine = Mesh(mesh.devices.reshape(4, 4, 4, 2, 2), names)
    placed = P(names[:2], names[2:], None, None)
    in_specs = (placed, P(names[:2]), P(), P())

    return jax.shard_map(on_device, mesh=fine, in_specs=in_specs, out_specs=placed, check_vma=False)
```
